32 devices in a mesh: parts: 2 (over y), row: 8 (over z, x), col: 2 (over core).
Axes of the slice: x: 2, y: 2, z: 4, core: 2. Of those that a mesh axis runs over, the one named last changes fastest.
Arguments:
- queries: bfloat16 [16384, 256], P(('parts', 'row', 'col')), parts along dimension 0, may hold values from -6 to 6
- counts: int32 [32], P(('parts', 'row', 'col')), parts along dimension 0, may hold values from 1 to 512, as said below
- memory: bfloat16 [512, 256], P(('parts', 'row', 'col')), parts along dimension 0, may hold values from -6 to 6
- mem_mask: int32 [512], P(('parts', 'row', 'col')), parts along dimension 0, may hold values from 0 to 1, as said below
- cross_wq: bfloat16 [256, 256], replicated, may hold values from -0.375 to 0.375
- cross_wkv: bfloat16 [256, 512], replicated, may hold values from -0.375 to 0.375
- cross_wo: bfloat16 [256, 256], replicated, may hold values from -0.375 to 0.375
- self_wqkv: bfloat16 [256, 768], replicated, may hold values from -0.375 to 0.375
- self_wo: bfloat16 [256, 256], replicated, may hold values from -0.375 to 0.375
- ffn_up: bfloat16 [256, 2048], replicated, may hold values from -0.375 to 0.375
- ffn_down: bfloat16 [2048, 256], replicated, may hold values from -0.125 to 0.125
- box_w1: bfloat16 [256, 256], replicated, may hold values from -0.375 to 0.375
- box_w2: bfloat16 [256, 256], replicated, may hold values from -0.375 to 0.375
- box_w3: bfloat16 [256, 4], replicated, may hold values from -0.375 to 0.375
- cross_temp: float32 [8], replicated, may hold values from 1 to 100
- self_temp: float32 [8], replicated, may hold values from 1 to 100
Outputs:
- features: float32 [16384, 256], P(('parts', 'row', 'col')), parts along dimension 0
- boxes: float32 [4, 16384], P(None, ('parts', 'row', 'col')), parts along dimension 1
The draws below stay inside these ranges and needn't reach their ends.
There are 2 independent parts, one for each index of `parts`. The reference program is written for one: setup_inputs(seed, part) draws one part's arguments, and reference() takes and returns one part's arrays. A program takes and returns all parts, laid end to end along the dimension named above; an argument that names none is the same for every part. Nothing has to cross between parts.
Inputs may be any that keep to these rules, and one draw needn't show every extreme that they name: The first counts[t] slots of tile t are live; some tile is full. `mem_mask`: the first memory token of every tile is live.
All inputs are finite; a program needn't handle non-finite values.
Results may differ from the reference program's by a relative error of at most 0.038.
The reference program's roundings to bfloat16 on the way (of `qc`, `kvm`, `ctx`, `qkv`, `sctx`, `upper` and `b2`) count: a program that leaves them out, or rounds other values in their place, can miss the bound.
Values may be sent and summed in bfloat16 or wider, within the bound.
A program may use at most 64 MiB of HBM per device.

```python
import math
import jax
import jax.numpy as jnp
from jax import lax

D = 256
HEADS = 8
FF = 2048
Q_DEV = 512
M_DEV = 16
TILES = 16
NQ = 8192
MEM = 256
N_ROW = 8
N_COL = 2


def draw_counts(key, part):
    first = jax.random.fold_in(key, 11)
    second = jax.random.fold_in(key, 12)
    values = jax.random.randint(first, (TILES,), 1, Q_DEV + 1)
    full_tile = jax.random.randint(second, (), 0, TILES)
    return jnp.where(jnp.arange(TILES) == full_tile, Q_DEV, values).astype(jnp.int32)


def draw_mem_mask(key, part):
    bits = jax.random.randint(jax.random.fold_in(key, 21), (MEM,), 0, 4)
    first = jnp.arange(MEM) % M_DEV == 0
    return jnp.where((bits > 0) | first, 1, 0).astype(jnp.int32)


def temper(key, salt):
    spread = jax.random.uniform(jax.random.fold_in(key, salt), (HEADS,), jnp.float32)
    high = jnp.full((HEADS,), math.log(6.0), jnp.float32)
    return jnp.exp(spread * high).astype(jnp.float32)


def draw_cross_temp(key, part):
    return temper(key, 31)


def draw_self_temp(key, part):
    return temper(key, 41)


def level_of(own_key, shape, cuts, low, top_value):
    def one(position, parts):
        heights = jax.random.uniform(jax.random.fold_in(jax.random.fold_in(own_key, 6), position), (parts,), jnp.float32, low / len(cuts), top_value / len(cuts))
        return jnp.repeat(jnp.exp(heights), shape[position] // parts).reshape((-1,) + (1,) * (len(shape) - position - 1))

    gain = one(*cuts[0])
    for cut in cuts[1:]:
        gain = gain * one(*cut)
    return gain


def bell_draw(own_key, dims, scale, limit, pieces=(), held_as=jnp.bfloat16):
    array = jax.random.normal(own_key, dims, jnp.float32) * scale
    if len(pieces) > 0:
        array = level_of(own_key, dims, pieces, -0.22, 0.18) * array
    return jnp.clip(array, min=-limit, max=limit).astype(held_as)


def setup_inputs(seed: int = 0, part: int = 0) -> dict:
    splits = jax.random.split(jax.random.key(seed), 17)
    part_splits = jax.random.split(jax.random.fold_in(splits[16], part), 17)
    queries = bell_draw(part_splits[0], (NQ, D), 1.0, 6.0, ((0, 16),))
    counts = draw_counts(jax.random.fold_in(jax.random.fold_in(splits[16], part), 71), part)
    memory = bell_draw(part_splits[2], (MEM, D), 1.0, 6.0, ((0, 16),))
    mem_mask = draw_mem_mask(jax.random.fold_in(jax.random.fold_in(splits[16], part), 71), part)
    cross_wq = bell_draw(splits[4], (D, D), D ** -0.5, 0.375)
    cross_wkv = bell_draw(splits[5], (D, 2 * D), D ** -0.5, 0.375)
    cross_wo = bell_draw(splits[6], (D, D), D ** -0.5, 0.375)
    self_wqkv = bell_draw(splits[7], (D, 3 * D), D ** -0.5, 0.375)
    self_wo = bell_draw(splits[8], (D, D), D ** -0.5, 0.375)
    ffn_up = bell_draw(splits[9], (D, FF), D ** -0.5, 0.375)
    ffn_down = bell_draw(splits[10], (FF, D), FF ** -0.5, 0.125)
    box_w1 = bell_draw(splits[11], (D, D), D ** -0.5, 0.375)
    box_w2 = bell_draw(splits[12], (D, D), D ** -0.5, 0.375)
    box_w3 = bell_draw(splits[13], (D, 4), D ** -0.5, 0.375)
    cross_temp = draw_cross_temp(jax.random.fold_in(splits[16], 71), part)
    self_temp = draw_self_temp(jax.random.fold_in(splits[16], 71), part)
    return dict(queries=queries, counts=counts, memory=memory, mem_mask=mem_mask, cross_wq=cross_wq, cross_wkv=cross_wkv, cross_wo=cross_wo, self_wqkv=self_wqkv, self_wo=self_wo, ffn_up=ffn_up, ffn_down=ffn_down, box_w1=box_w1, box_w2=box_w2, box_w3=box_w3, cross_temp=cross_temp, self_temp=self_temp)


EPS = 1e-06

def rms_norm(x):
    return x * lax.rsqrt(lax.optimization_barrier(jnp.mean(x * x, axis=-1, keepdims=True)) + EPS)

def attend(query, keyval, live, scale):
    rows = query.shape[0]
    width = query.shape[1]
    heads = scale.shape[0]
    hsize = width // heads
    q3 = query.astype(jnp.float32).reshape(rows, heads, hsize)
    keys = keyval[:, :width].astype(jnp.float32).reshape(-1, heads, hsize)
    values = keyval[:, width:].astype(jnp.float32).reshape(-1, heads, hsize)
    scores = jnp.einsum('qhd,khd->hqk', q3, keys, precision=lax.Precision.HIGHEST) * scale[:, None, None]
    keep = (live > 0)[None, None, :]
    top = lax.optimization_barrier(jnp.max(jnp.where(keep, scores, -1e+30), axis=-1, keepdims=True))
    weights = jnp.where(keep, jnp.exp(scores - top), 0.0)
    total = lax.optimization_barrier(jnp.sum(weights, axis=-1))
    rounded = lax.optimization_barrier(weights.astype(jnp.bfloat16)).astype(jnp.float32)
    mixed = jnp.einsum('hqk,khd->qhd', rounded, values, precision=lax.Precision.HIGHEST)
    mixed = mixed / jnp.transpose(total)[:, :, None]
    return mixed.reshape(rows, width)

def reference(queries, counts, memory, mem_mask, cross_wq, cross_wkv, cross_wo, self_wqkv, self_wo, ffn_up, ffn_down, box_w1, box_w2, box_w3, cross_temp, self_temp):
    hsize = D // HEADS
    slots = jnp.arange(Q_DEV, dtype=jnp.int32)
    valid = (slots[None, :] < counts[:, None]).reshape(NQ)
    xres = queries.astype(jnp.float32)
    hn0 = rms_norm(xres).astype(jnp.bfloat16)
    qc = jnp.dot(hn0, cross_wq, preferred_element_type=jnp.float32).astype(jnp.bfloat16)
    kvm = jnp.dot(memory, cross_wkv, preferred_element_type=jnp.float32).astype(jnp.bfloat16)
    scale_c = cross_temp / jnp.sqrt(jnp.float32(hsize))
    q_tiles = qc.reshape(N_ROW, N_COL, Q_DEV, D)
    kv_tiles = kvm.reshape(N_ROW, N_COL, M_DEV, 2 * D)
    m_tiles = mem_mask.reshape(N_ROW, N_COL, M_DEV)
    columns = []
    for column in range(N_COL):
        strip = kv_tiles[:, column].reshape(N_ROW * M_DEV, 2 * D)
        strip_live = m_tiles[:, column].reshape(N_ROW * M_DEV)
        columns.append(lax.map(lambda q: attend(q, strip, strip_live, scale_c), q_tiles[:, column]))
    ctx = jnp.stack(columns, axis=1).reshape(NQ, D)
    ctx = jnp.where(valid[:, None], ctx, 0.0).astype(jnp.bfloat16)
    x1 = xres + jnp.dot(ctx, cross_wo, preferred_element_type=jnp.float32)
    hn1 = rms_norm(x1).astype(jnp.bfloat16)
    qkv = jnp.dot(hn1, self_wqkv, preferred_element_type=jnp.float32).astype(jnp.bfloat16)
    scale_s = self_temp / jnp.sqrt(jnp.float32(hsize))
    row_qkv = qkv.reshape(N_ROW, N_COL * Q_DEV, 3 * D)
    row_live = valid.astype(jnp.int32).reshape(N_ROW, N_COL * Q_DEV)

    def self_row(pair):
        block, live = pair
        return attend(block[:, :D], block[:, D:], live, scale_s)
    sctx = lax.map(self_row, (row_qkv, row_live)).reshape(NQ, D)
    sctx = jnp.where(valid[:, None], sctx, 0.0).astype(jnp.bfloat16)
    x2 = x1 + jnp.dot(sctx, self_wo, preferred_element_type=jnp.float32)
    hn2 = rms_norm(x2).astype(jnp.bfloat16)
    upper = jnp.maximum(jnp.dot(hn2, ffn_up, preferred_element_type=jnp.float32), 0.0).astype(jnp.bfloat16)
    x3 = x2 + jnp.dot(upper, ffn_down, preferred_element_type=jnp.float32)
    features = jnp.where(valid[:, None], x3, 0.0).astype(jnp.float32)
    hn3 = rms_norm(x3).astype(jnp.bfloat16)
    b1 = jnp.maximum(jnp.dot(hn3, box_w1, preferred_element_type=jnp.float32), 0.0).astype(jnp.bfloat16)
    b2 = jnp.maximum(jnp.dot(b1, box_w2, preferred_element_type=jnp.float32), 0.0).astype(jnp.bfloat16)
    raw_box = jax.nn.sigmoid(jnp.dot(b2, box_w3, preferred_element_type=jnp.float32))
    boxes = jnp.transpose(jnp.where(valid[:, None], raw_box, 0.0))
    return (features, boxes)
```

```python
import functools
import math

import jax
import jax.numpy as jnp
from jax import lax
from jax.experimental import pallas as pl
from jax.experimental.pallas import tpu as pltpu
from jax.sharding import PartitionSpec as P

EPS = 1e-06
LANES = 128
TAIL = 16
BF = jnp.bfloat16
F32 = jnp.float32
MESH = pl.DeviceIdType.MESH
DEAD = 64.0


def rms_round(x):
    return (x * lax.rsqrt(jnp.mean(x * x, axis=-1, keepdims=True) + EPS)).astype(BF)


def mm(a, b):
    return jnp.dot(a, b, preferred_element_type=F32)


def mm_t(a, b):
    return lax.dot_general(a, b, (((1,), (1,)), ((), ())), preferred_element_type=F32)


def flip(x):
    return x.astype(F32).T.astype(BF)


def each(n, body):
    if n <= 16:
        for i in range(n):
            body(i)
    else:
        lax.fori_loop(0, n, lambda i, c: (body(i), c)[1], 0)


def twice(w, hsize):
    pair = 2 * hsize
    return jnp.concatenate([w[:, i : i + pair] for i in range(0, w.shape[1], pair) for _ in (0, 1)], axis=1)


def put_queries(w_ref, qt, temp_ref, hsize):
    zero = jnp.zeros((hsize, qt.shape[1]), BF)
    for h in range(w_ref.shape[0]):
        x = qt[h * hsize : (h + 1) * hsize].astype(BF).astype(F32)
        x = x * (temp_ref[h] * (math.log2(math.e) / math.sqrt(hsize)))
        hi = x.astype(BF)
        lo = (x - hi.astype(F32)).astype(BF)
        for j in (0, 1):
            mine = h % 2 == j
            w_ref[h, j * hsize : (j + 1) * hsize, :] = hi if mine else zero
            w_ref[h, (2 + j) * hsize : (3 + j) * hsize, :] = lo if mine else zero


def put_keys(ka_ref, k, live, first):
    for g in range(k.shape[1] // LANES):
        lanes = slice(g * LANES, (g + 1) * LANES)
        ka_ref[g] = jnp.where(live, k[:, lanes], first[:, lanes]).astype(BF)


def put_values(vt_ref, vt, live, hsize):
    flags = jnp.broadcast_to(live.astype(F32), (TAIL, vt.shape[1])).astype(BF)
    for h in range(vt_ref.shape[0]):
        vt_ref[h, :hsize, :] = jnp.where(live, vt[h * hsize : (h + 1) * hsize], 0.0).astype(BF)
        vt_ref[h, hsize:, :] = flags


def attend(w_ref, chunks, s_v, e_v, m_v, rows, put):
    heads = w_ref.shape[0]
    for u in range(heads + 2):
        a, b = u % 2, (u + 1) % 2
        best = total = None
        if 1 <= u <= heads:
            top = jnp.max(m_v[b, :, :rows], axis=0, keepdims=True)
        at = 0
        for keys_of, values_of, size in chunks:
            here = slice(at, at + size)
            at += size
            if u < heads:
                s = mm(keys_of(u // 2), w_ref[u, :, :rows])
                s_v[a, here, :rows] = s
                part = jnp.max(s.reshape(size // 8, 8, rows), axis=0)
                best = part if best is None else jnp.maximum(best, part)
            if 1 <= u <= heads:
                e_v[b, here, :rows] = jnp.exp2(s_v[b, here, :rows] - top).astype(BF)
            if u >= 2:
                part = mm(values_of(u - 2), e_v[a, here, :rows])
                total = part if total is None else total + part
        if u < heads:
            m_v[a, :, :rows] = best
        if u >= 2:
            put(u - 2, total)


def mixer(
    n_row, hsize, tm,
    q_hbm, cnt_s, mem_hbm, mask_h, wq_h, wkv_h, wo_h, wqkv_h, swo_h, up_h, down_h, w1_h, w2_h, w3_h, ct_h, st_h,
    x1_v, ws, kas, vts, cnt, swo, up, down, w1, w2, w3,
    q_v, wq, wkv, wo, wqkv,
    mask_s, ct_s, st_s, mem_v, gat, wc, kac, vtc, ctx_v, hn_v, hn_o, s_v, e_v, m_v, ckw, cvw, skw, sqw,
    in_sem, gsend, grecv, csend, crecv, hsend, hrecv, msem,
):
    n, width = q_v.shape
    m_dev = mem_hbm.shape[0]
    row = lax.axis_index("row")
    other = 1 - lax.axis_index("col")

    barrier = pltpu.get_barrier_semaphore()

    def greet(i):
        pl.semaphore_signal(
            barrier, inc=1, device_id={"row": lax.rem(row + 1 + i, n_row)}, device_id_type=MESH
        )

    each(n_row - 1, greet)
    pl.semaphore_signal(barrier, inc=1, device_id={"col": other}, device_id_type=MESH)

    small = [
        pltpu.make_async_copy(a, b, msem.at[i])
        for i, (a, b) in enumerate(
            ((mem_hbm, mem_v), (mask_h, mask_s), (ct_h, ct_s), (st_h, st_s))
        )
    ]
    for load in small:
        load.start()
    pairs = (
        (q_hbm, q_v), (wq_h, wq), (wkv_h, wkv), (wo_h, wo), (wqkv_h, wqkv),
        (swo_h, swo), (up_h, up), (down_h, down), (w1_h, w1), (w2_h, w2), (w3_h, w3),
    )
    loads = [pltpu.make_async_copy(a, b, in_sem.at[i]) for i, (a, b) in enumerate(pairs)]
    for load in loads:
        load.start()

    for load in small:
        load.wait()
    slot = lax.broadcasted_iota(jnp.int32, (m_dev, width), 0)
    flags = jnp.zeros((m_dev, width), jnp.int32)
    for i in range(m_dev):
        flags = jnp.where(slot == i, mask_s[i], flags)
    gat[row] = jnp.where(flags > 0, mem_v[...].astype(F32), DEAD).astype(BF)
    count = cnt_s[0]
    cnt[0] = jnp.full((8, LANES), count, jnp.int32)
    pl.semaphore_wait(barrier, n_row)

    def gather_copy(i):
        return pltpu.make_async_remote_copy(
            src_ref=gat.at[row], dst_ref=gat.at[row],
            send_sem=gsend.at[i], recv_sem=grecv.at[row],
            device_id={"row": lax.rem(row + 1 + i, n_row)}, device_id_type=MESH,
        )

    each(n_row - 1, lambda i: gather_copy(i).start())
    count_copy = pltpu.make_async_remote_copy(
        src_ref=cnt.at[0], dst_ref=cnt.at[1], send_sem=csend, recv_sem=crecv,
        device_id={"col": other}, device_id_type=MESH,
    )
    count_copy.start()

    loads[0].wait()
    loads[1].wait()
    qct = mm_t(flip(wq[...]), rms_round(q_v[...].astype(F32)))
    put_queries(wc, qct, ct_s, hsize)
    loads[2].wait()
    ckw[...] = twice(wkv[:, :width].astype(F32), hsize).astype(BF)
    cvw[...] = flip(wkv[:, width:])
    loads[4].wait()
    skw[...] = twice(wqkv[:, width : 2 * width].astype(F32), hsize).astype(BF)
    sqw[:width] = flip(wqkv[:, :width])
    sqw[width:] = flip(wqkv[:, 2 * width :])
    loads[3].wait()

    def arrived(i):
        j = lax.rem(row + 1 + i, n_row)
        pltpu.make_async_remote_copy(
            src_ref=gat.at[j], dst_ref=gat.at[j],
            send_sem=gsend.at[i], recv_sem=grecv.at[j],
            device_id={"row": j}, device_id_type=MESH,
        ).wait_recv()

    each(n_row - 1, arrived)

    keys = n_row * m_dev
    held = gat[...].reshape(keys, width)
    marks = held[:, :LANES].astype(F32)
    k = mm(held, ckw[...])
    put_keys(kac, k, marks < 0.5 * DEAD, k[0:1])
    put_values(vtc, mm_t(cvw[...], held), marks.T[0:1] < 0.5 * DEAD, hsize)

    size = min(512, keys)
    chunks = [
        (
            lambda g, at=at: kac[g, at : at + size],
            lambda h, at=at: vtc[h, :, at : at + size],
            size,
        )
        for at in range(0, keys, size)
    ]
    lane = lax.broadcasted_iota(jnp.int32, (1, n), 1)

    def put_ctx(h, total):
        part = total[:hsize] / total[hsize : hsize + 1]
        ctx_v[h * hsize : (h + 1) * hsize, :] = jnp.where(lane < count, part, 0.0)

    attend(wc, chunks, s_v, e_v, m_v, n, put_ctx)

    def hn_copy(t):
        rows = pl.ds(t * tm, tm)
        return pltpu.make_async_remote_copy(
            src_ref=hn_v.at[rows], dst_ref=hn_o.at[rows],
            send_sem=hsend.at[t], recv_sem=hrecv.at[t],
            device_id={"col": other}, device_id_type=MESH,
        )

    for t in range(n // tm):
        rows = slice(t * tm, (t + 1) * tm)
        ctx = ctx_v[:, rows].T.astype(BF)
        x1 = q_v[rows, :].astype(F32) + mm(ctx, wo[...])
        x1_v[rows, :] = x1
        hn_v[rows, :] = rms_round(x1)
        hn_copy(t).start()

    k = mm(hn_v[...], skw[...])
    first = k[0:1]
    spot = lax.broadcasted_iota(jnp.int32, (n, LANES), 0)
    put_keys(kas.at[0], k, spot < count, first)
    qvt = mm_t(sqw[...], hn_v[...])
    put_queries(ws, qvt[:width], st_s, hsize)
    put_values(vts.at[0], qvt[width:], lane < count, hsize)
    count_copy.wait()
    for t in range(n // tm):
        hn_copy(t).wait()
    theirs = cnt[1, 0:1, :]
    put_keys(kas.at[1], mm(hn_o[...], skw[...]), spot < theirs, first)
    put_values(vts.at[1], mm_t(sqw[width:], hn_o[...]), lane < theirs[:, 0:1], hsize)

    for load in loads[5:]:
        load.wait()
    each(n_row - 1, lambda i: gather_copy(i).wait_send())


def reader(
    hsize,
    x1_v, ws, kas, vts, cnt, swo, up, down, w1, w2, w3,
    feat_ref, box_ref,
    sc_v, out_v, box_v, s_v, e_v, m_v, sems,
):
    n, width = x1_v.shape
    count = jnp.max(cnt[0])
    theirs = jnp.max(cnt[1])
    unit = min(LANES, n)
    half = n // 2
    more = (theirs > count).astype(jnp.int32)
    fewer = jnp.minimum(theirs, count)
    lane = lax.broadcasted_iota(jnp.int32, (1, n), 1)

    def self_rows(rows, size):
        def side(s, upto):
            return (lambda g: kas[s, g, :upto], lambda h: vts[s, h, :, :upto], upto)

        def put(h, total):
            part = total[:hsize] / total[hsize : hsize + 1]
            sc_v[h * hsize : (h + 1) * hsize, :rows] = jnp.where(lane[:, :rows] < count, part, 0.0)

        attend(ws, [side(more, n), side(1 - more, size)], s_v, e_v, m_v, rows, put)

    @pl.when(count <= half)
    def _():
        sc_v[:, half:] = jnp.zeros((width, n - half), F32)

    for i in range(n // unit):
        size = (i + 1) * unit
        chosen = (fewer - 1) // unit == i

        @pl.when(jnp.logical_and(chosen, count > half))
        def _():
            self_rows(n, size)

        if size % (2 * unit) == 0:

            @pl.when(jnp.logical_and((fewer - 1) // (2 * unit) == i // 2, count <= half))
            def _():
                self_rows(half, size)

    x2 = x1_v[...] + mm(sc_v[...].T.astype(BF), swo[...])
    hn2 = rms_round(x2)
    ff = up.shape[1]
    step = min(512, ff)
    x3 = x2
    for f in range(0, ff, step):
        upper = jnp.maximum(mm(hn2, up[:, f : f + step]), 0.0).astype(BF)
        x3 = x3 + mm(upper, down[f : f + step, :])
    alive = lax.broadcasted_iota(jnp.int32, (n, width), 0) < count
    out_v[...] = jnp.where(alive, x3, 0.0)
    put = pltpu.make_async_copy(out_v, feat_ref, sems.at[0])
    put.start()
    hn3 = rms_round(x3)
    b1 = jnp.maximum(mm(hn3, w1[...]), 0.0).astype(BF)
    b2 = jnp.maximum(mm(b1, w2[...]), 0.0).astype(BF)
    z = lax.dot_general(w3[...], b2, (((1,), (1,)), ((), ())), preferred_element_type=F32)
    box = 1.0 / (1.0 + jnp.exp(-z))
    box_v[...] = jnp.where(lax.broadcasted_iota(jnp.int32, box.shape, 1) < count, box, 0.0)
    put_box = pltpu.make_async_copy(box_v, box_ref, sems.at[1])
    put_box.start()
    put.wait()
    put_box.wait()


def pin(x):
    return pltpu.with_memory_space_constraint(x, pltpu.HBM)


def local(n_row, *args):
    queries, counts, memory, mem_mask = args[:4]
    weights = args[4:13] + (args[13].T,)
    n, width = queries.shape
    m_dev = memory.shape[0]
    heads = args[14].shape[0]
    hsize = width // heads
    keys = n_row * m_dev
    groups = 2 * width // LANES
    tm = min(256, n)
    hbm = pl.BlockSpec(memory_space=pltpu.HBM)
    smem = pl.BlockSpec(memory_space=pltpu.SMEM)
    vmem = pl.BlockSpec(memory_space=pltpu.VMEM)
    dma = pltpu.SemaphoreType.DMA
    boxes = weights[-1].shape[0]
    like = jax.ShapeDtypeStruct
    held = pl.pallas_call(
        functools.partial(mixer, n_row, hsize, tm),
        out_shape=(
            like((n, width), F32),
            like((heads, LANES, n), BF),
            like((2, groups, n, LANES), BF),
            like((2, heads, hsize + TAIL, n), BF),
            like((2, 8, LANES), jnp.int32),
        )
        + tuple(like(w.shape, BF) for w in weights[4:]),
        in_specs=[hbm, smem] + [hbm] * 14,
        out_specs=(vmem,) * (5 + len(weights[4:])),
        scratch_shapes=[pltpu.VMEM(queries.shape, BF)]
        + [pltpu.VMEM(w.shape, BF) for w in weights[:4]]
        + [
            pltpu.SMEM(mem_mask.shape, jnp.int32),
            pltpu.SMEM((heads,), F32),
            pltpu.SMEM((heads,), F32),
            pltpu.VMEM(memory.shape, BF),
            pltpu.VMEM((n_row, m_dev, width), BF),
            pltpu.VMEM((heads, LANES, n), BF),
            pltpu.VMEM((groups, keys, LANES), BF),
            pltpu.VMEM((heads, hsize + TAIL, keys), BF),
            pltpu.VMEM((width, n), F32),
            pltpu.VMEM((n, width), BF),
            pltpu.VMEM((n, width), BF),
            pltpu.VMEM((2, keys, n), F32),
            pltpu.VMEM((2, keys, n), BF),
            pltpu.VMEM((2, 8, n), F32),
            pltpu.VMEM((width, 2 * width), BF),
            pltpu.VMEM((width, width), BF),
            pltpu.VMEM((width, 2 * width), BF),
            pltpu.VMEM((2 * width, width), BF),
            dma((11,)),
            dma((n_row - 1,)),
            dma((n_row,)),
            dma,
            dma,
            dma((n // tm,)),
            dma((n // tm,)),
            dma((4,)),
        ],
        compiler_params=pltpu.CompilerParams(
            collective_id=0, has_side_effects=True, vmem_limit_bytes=40 * 1024 * 1024
        ),
        name="mixer",
    )(pin(queries), counts, *map(pin, args[2:4] + weights + args[14:]))
    return pl.pallas_call(
        functools.partial(reader, hsize),
        out_shape=(like((n, width), F32), like((boxes, n), F32)),
        in_specs=[vmem] * 11,
        out_specs=(hbm, hbm),
        scratch_shapes=[
            pltpu.VMEM((width, n), F32),
            pltpu.VMEM((n, width), F32),
            pltpu.VMEM((boxes, n), F32),
            pltpu.VMEM((2, 2 * n, n), F32),
            pltpu.VMEM((2, 2 * n, n), BF),
            pltpu.VMEM((2, 8, n), F32),
            dma((2,)),
        ],
        compiler_params=pltpu.CompilerParams(vmem_limit_bytes=32 * 1024 * 1024),
        name="reader",
    )(*held)


def solution(mesh):
    spread = ("parts", "row", "col")
    return jax.shard_map(
        functools.partial(local, mesh.shape["row"]),
        mesh=mesh,
        in_specs=(P(spread, None), P(spread), P(spread, None), P(spread)) + (P(),) * 12,
        out_specs=(P(spread, None), P(None, spread)),
        check_vma=False,
    )
```

```python
import functools
import math

import jax
import jax.numpy as jnp
from jax import lax
from jax.experimental import pallas as pl
from jax.experimental.pallas import tpu as pltpu
from jax.sharding import PartitionSpec as P

EPS = 1e-06
LANES = 128
TAIL = 16
BF = jnp.bfloat16
F32 = jnp.float32
MESH = pl.DeviceIdType.MESH
DEAD = 64.0


def rms_round(x):
    return (x * lax.rsqrt(jnp.mean(x * x, axis=-1, keepdims=True) + EPS)).astype(BF)


def mm(a, b):
    return jnp.dot(a, b, preferred_element_type=F32)


def mm_t(a, b):
    return lax.dot_general(a, b, (((1,), (1,)), ((), ())), preferred_element_type=F32)


def flip(x):
    return x.astype(F32).T.astype(BF)


def each(n, body):
    if n <= 16:
        for i in range(n):
            body(i)
    else:
        lax.fori_loop(0, n, lambda i, c: (body(i), c)[1], 0)


def twice(w, hsize):
    pair = 2 * hsize
    return jnp.concatenate([w[:, i : i + pair] for i in range(0, w.shape[1], pair) for _ in (0, 1)], axis=1)


def put_queries(w_ref, qt, temp_ref, hsize):
    zero = jnp.zeros((hsize, qt.shape[1]), BF)
    for h in range(w_ref.shape[0]):
        x = qt[h * hsize : (h + 1) * hsize].astype(BF).astype(F32)
        x = x * (temp_ref[h] * (math.log2(math.e) / math.sqrt(hsize)))
        hi = x.astype(BF)
        lo = (x - hi.astype(F32)).astype(BF)
        for j in (0, 1):
            mine = h % 2 == j
            w_ref[h, j * hsize : (j + 1) * hsize, :] = hi if mine else zero
            w_ref[h, (2 + j) * hsize : (3 + j) * hsize, :] = lo if mine else zero


def put_keys(ka_ref, k, live, first):
    for g in range(k.shape[1] // LANES):
        lanes = slice(g * LANES, (g + 1) * LANES)
        ka_ref[g] = jnp.where(live, k[:, lanes], first[:, lanes]).astype(BF)


def put_values(vt_ref, vt, live, hsize):
    flags = jnp.broadcast_to(live.astype(F32), (TAIL, vt.shape[1])).astype(BF)
    for h in range(vt_ref.shape[0]):
        vt_ref[h, :hsize, :] = jnp.where(live, vt[h * hsize : (h + 1) * hsize], 0.0).astype(BF)
        vt_ref[h, hsize:, :] = flags


def attend(w_ref, chunks, tile, tiles, put, refs=(None, None, None)):
    heads = w_ref.shape[0]
    units = [(t, h) for t in range(tiles) for h in range(heads)]
    held = {}

    def keep(kind, u, here, x):
        if refs[kind] is None:
            held[kind, u, here.start] = x
        else:
            refs[kind][u % 2, here] = x

    def back(kind, u, here):
        return held.pop((kind, u, here.start)) if refs[kind] is None else refs[kind][u % 2, here]

    eight = slice(0, 8)
    for u in range(len(units) + 2):
        best = total = None
        if 1 <= u <= len(units):
            top = jnp.max(back(2, u - 1, eight), axis=0, keepdims=True)
        at = 0
        for keys_of, values_of, size in chunks:
            here = slice(at, at + size)
            at += size
            if u < len(units):
                t, h = units[u]
                s = mm(keys_of(h // 2), w_ref[h, :, t * tile : (t + 1) * tile])
                keep(0, u, here, s)
                part = jnp.max(s.reshape(size // 8, 8, tile), axis=0)
                best = part if best is None else jnp.maximum(best, part)
            if 1 <= u <= len(units):
                keep(1, u - 1, here, jnp.exp2(back(0, u - 1, here) - top).astype(BF))
            if u >= 2:
                part = mm(values_of(units[u - 2][1]), back(1, u - 2, here))
                total = part if total is None else total + part
        if u < len(units):
            keep(2, u, eight, best)
        if u >= 2:
            put(*units[u - 2], total)


def mixer(
    n_row, hsize,
    q_hbm, cnt_s, mem_hbm, mask_h, wq_h, wkv_h, wo_h, wqkv_h, swo_h, up_h, down_h, w1_h, w2_h, w3_h, ct_h, st_h,
    x1_v, ws, kas, vts, cnt, swo, up, down, w1, w2, w3,
    q_v, wq, wkv, wo, wqkv,
    mask_s, ct_s, st_s, mem_v, gat, wc, kac, vtc, ctx_v, hn_v, hn_o, s_v, e_v, m_v, ckw, cvw, skw, sqw,
    in_sem, gsend, grecv, csend, crecv, hsend, hrecv, msem,
):
    n, width = q_v.shape
    m_dev = mem_hbm.shape[0]
    row = lax.axis_index("row")
    other = 1 - lax.axis_index("col")

    barrier = pltpu.get_barrier_semaphore()

    def greet(i):
        pl.semaphore_signal(
            barrier, inc=1, device_id={"row": lax.rem(row + 1 + i, n_row)}, device_id_type=MESH
        )

    each(n_row - 1, greet)
    pl.semaphore_signal(barrier, inc=1, device_id={"col": other}, device_id_type=MESH)

    small = [
        pltpu.make_async_copy(a, b, msem.at[i])
        for i, (a, b) in enumerate(
            ((mem_hbm, mem_v), (mask_h, mask_s), (ct_h, ct_s), (st_h, st_s))
        )
    ]
    for load in small:
        load.start()
    pairs = (
        (q_hbm, q_v), (wq_h, wq), (wkv_h, wkv), (wo_h, wo), (wqkv_h, wqkv),
        (swo_h, swo), (up_h, up), (down_h, down), (w1_h, w1), (w2_h, w2), (w3_h, w3),
    )
    loads = [pltpu.make_async_copy(a, b, in_sem.at[i]) for i, (a, b) in enumerate(pairs)]
    for load in loads:
        load.start()

    for load in small:
        load.wait()
    slot = lax.broadcasted_iota(jnp.int32, (m_dev, width), 0)
    flags = jnp.zeros((m_dev, width), jnp.int32)
    for i in range(m_dev):
        flags = jnp.where(slot == i, mask_s[i], flags)
    gat[row] = jnp.where(flags > 0, mem_v[...].astype(F32), DEAD).astype(BF)
    count = cnt_s[0]
    cnt[0] = jnp.full((8, LANES), count, jnp.int32)
    pl.semaphore_wait(barrier, n_row)

    def gather_copy(i):
        return pltpu.make_async_remote_copy(
            src_ref=gat.at[row], dst_ref=gat.at[row],
            send_sem=gsend.at[i], recv_sem=grecv.at[row],
            device_id={"row": lax.rem(row + 1 + i, n_row)}, device_id_type=MESH,
        )

    each(n_row - 1, lambda i: gather_copy(i).start())
    count_copy = pltpu.make_async_remote_copy(
        src_ref=cnt.at[0], dst_ref=cnt.at[1], send_sem=csend, recv_sem=crecv,
        device_id={"col": other}, device_id_type=MESH,
    )
    count_copy.start()

    loads[0].wait()
    loads[1].wait()
    qct = mm_t(flip(wq[...]), rms_round(q_v[...].astype(F32)))
    put_queries(wc, qct, ct_s, hsize)
    loads[2].wait()
    ckw[...] = twice(wkv[:, :width].astype(F32), hsize).astype(BF)
    cvw[...] = flip(wkv[:, width:])
    loads[4].wait()
    skw[...] = twice(wqkv[:, width : 2 * width].astype(F32), hsize).astype(BF)
    sqw[:width] = flip(wqkv[:, :width])
    sqw[width:] = flip(wqkv[:, 2 * width :])
    loads[3].wait()

    def arrived(i):
        j = lax.rem(row + 1 + i, n_row)
        pltpu.make_async_remote_copy(
            src_ref=gat.at[j], dst_ref=gat.at[j],
            send_sem=gsend.at[i], recv_sem=grecv.at[j],
            device_id={"row": j}, device_id_type=MESH,
        ).wait_recv()

    each(n_row - 1, arrived)

    keys = n_row * m_dev
    held = gat[...].reshape(keys, width)
    marks = held[:, :LANES].astype(F32)
    k = mm(held, ckw[...])
    put_keys(kac, k, marks < 0.5 * DEAD, k[0:1])
    put_values(vtc, mm_t(cvw[...], held), marks.T[0:1] < 0.5 * DEAD, hsize)

    size = min(512, keys)
    chunks = [
        (
            lambda g, at=at: kac[g, at : at + size],
            lambda h, at=at: vtc[h, :, at : at + size],
            size,
        )
        for at in range(0, keys, size)
    ]
    lane = lax.broadcasted_iota(jnp.int32, (1, n), 1)

    per = LANES // hsize
    parts = []

    def put_ctx(t, h, total):
        part = total[:hsize] / total[hsize : hsize + 1]
        parts.append(jnp.where(lane < count, part, 0.0))
        if len(parts) == per:
            ctx_v[:, (h - per + 1) * hsize : (h + 1) * hsize] = jnp.concatenate(parts, axis=0).T.astype(BF)
            parts.clear()

    attend(wc, chunks, n, 1, put_ctx, (s_v, e_v, m_v))

    x1 = q_v[...].astype(F32) + mm(ctx_v[...], wo[...])
    hn_v[...] = rms_round(x1)
    hn_copy = pltpu.make_async_remote_copy(
        src_ref=hn_v, dst_ref=hn_o, send_sem=hsend, recv_sem=hrecv,
        device_id={"col": other}, device_id_type=MESH,
    )
    hn_copy.start()
    x1_v[...] = x1

    k = mm(hn_v[...], skw[...])
    first = k[0:1]
    spot = lax.broadcasted_iota(jnp.int32, (n, LANES), 0)
    put_keys(kas.at[0], k, spot < count, first)
    qvt = mm_t(sqw[...], hn_v[...])
    put_queries(ws, qvt[:width], st_s, hsize)
    put_values(vts.at[0], qvt[width:], lane < count, hsize)
    count_copy.wait()
    hn_copy.wait_recv()
    theirs = cnt[1, 0:1, :]
    put_keys(kas.at[1], mm(hn_o[...], skw[...]), spot < theirs, first)
    put_values(vts.at[1], mm_t(sqw[width:], hn_o[...]), lane < theirs[:, 0:1], hsize)

    for load in loads[5:]:
        load.wait()
    each(n_row - 1, lambda i: gather_copy(i).wait_send())
    hn_copy.wait_send()


def reader(
    hsize,
    x1_v, ws, kas, vts, cnt, swo, up, down, w1, w2, w3,
    feat_ref, box_ref,
    sc_v, out_v, box_v, sems,
):
    n, width = x1_v.shape
    heads = ws.shape[0]
    count = jnp.max(cnt[0])
    theirs = jnp.max(cnt[1])
    unit = min(LANES, n)
    half = n // 2
    more = (theirs > count).astype(jnp.int32)
    fewer = jnp.minimum(theirs, count)
    lane = lax.broadcasted_iota(jnp.int32, (1, n), 1)

    def self_rows(rows, size):
        def side(s, upto):
            return (lambda g: kas[s, g, :upto], lambda h: vts[s, h, :, :upto], upto)

        parts = []

        def put(t, h, total):
            parts.append(total[:hsize] / total[hsize : hsize + 1])
            if h == heads - 1:
                here = slice(t * unit, (t + 1) * unit)
                whole = jnp.where(lane[:, here] < count, jnp.concatenate(parts, axis=0), 0.0)
                sc_v[here, :] = whole.T.astype(BF)
                parts.clear()

        attend(ws, [side(more, n), side(1 - more, size)], unit, rows // unit, put)

    @pl.when(count <= half)
    def _():
        sc_v[half:, :] = jnp.zeros((n - half, width), BF)

    for i in range(n // unit):
        size = (i + 1) * unit
        chosen = (fewer - 1) // unit == i

        @pl.when(jnp.logical_and(chosen, count > half))
        def _():
            self_rows(n, size)

        if size % (2 * unit) == 0:

            @pl.when(jnp.logical_and((fewer - 1) // (2 * unit) == i // 2, count <= half))
            def _():
                self_rows(half, size)

    x2 = x1_v[...] + mm(sc_v[...], swo[...])
    hn2 = rms_round(x2)
    ff = up.shape[1]
    step = min(512, ff)
    x3 = x2
    for f in range(0, ff, step):
        upper = jnp.maximum(mm(hn2, up[:, f : f + step]), 0.0).astype(BF)
        x3 = x3 + mm(upper, down[f : f + step, :])
    alive = lax.broadcasted_iota(jnp.int32, (n, width), 0) < count
    out_v[...] = jnp.where(alive, x3, 0.0)
    put = pltpu.make_async_copy(out_v, feat_ref, sems.at[0])
    put.start()
    hn3 = rms_round(x3)
    b1 = jnp.maximum(mm(hn3, w1[...]), 0.0).astype(BF)
    b2 = jnp.maximum(mm(b1, w2[...]), 0.0).astype(BF)
    z = lax.dot_general(w3[...], b2, (((1,), (1,)), ((), ())), preferred_element_type=F32)
    box = 1.0 / (1.0 + jnp.exp(-z))
    box_v[...] = jnp.where(lax.broadcasted_iota(jnp.int32, box.shape, 1) < count, box, 0.0)
    put_box = pltpu.make_async_copy(box_v, box_ref, sems.at[1])
    put_box.start()
    put.wait()
    put_box.wait()


def pin(x):
    return pltpu.with_memory_space_constraint(x, pltpu.HBM)


def local(n_row, *args):
    queries, counts, memory, mem_mask = args[:4]
    weights = args[4:13] + (args[13].T,)
    n, width = queries.shape
    m_dev = memory.shape[0]
    heads = args[14].shape[0]
    hsize = width // heads
    keys = n_row * m_dev
    groups = 2 * width // LANES
    hbm = pl.BlockSpec(memory_space=pltpu.HBM)
    smem = pl.BlockSpec(memory_space=pltpu.SMEM)
    vmem = pl.BlockSpec(memory_space=pltpu.VMEM)
    dma = pltpu.SemaphoreType.DMA
    boxes = weights[-1].shape[0]
    like = jax.ShapeDtypeStruct
    held = pl.pallas_call(
        functools.partial(mixer, n_row, hsize),
        out_shape=(
            like((n, width), F32),
            like((heads, LANES, n), BF),
            like((2, groups, n, LANES), BF),
            like((2, heads, hsize + TAIL, n), BF),
            like((2, 8, LANES), jnp.int32),
        )
        + tuple(like(w.shape, BF) for w in weights[4:]),
        in_specs=[hbm, smem] + [hbm] * 14,
        out_specs=(vmem,) * (5 + len(weights[4:])),
        scratch_shapes=[pltpu.VMEM(queries.shape, BF)]
        + [pltpu.VMEM(w.shape, BF) for w in weights[:4]]
        + [
            pltpu.SMEM(mem_mask.shape, jnp.int32),
            pltpu.SMEM((heads,), F32),
            pltpu.SMEM((heads,), F32),
            pltpu.VMEM(memory.shape, BF),
            pltpu.VMEM((n_row, m_dev, width), BF),
            pltpu.VMEM((heads, LANES, n), BF),
            pltpu.VMEM((groups, keys, LANES), BF),
            pltpu.VMEM((heads, hsize + TAIL, keys), BF),
            pltpu.VMEM((n, width), BF),
            pltpu.VMEM((n, width), BF),
            pltpu.VMEM((n, width), BF),
            pltpu.VMEM((2, keys, n), F32),
            pltpu.VMEM((2, keys, n), BF),
            pltpu.VMEM((2, 8, n), F32),
            pltpu.VMEM((width, 2 * width), BF),
            pltpu.VMEM((width, width), BF),
            pltpu.VMEM((width, 2 * width), BF),
            pltpu.VMEM((2 * width, width), BF),
            dma((11,)),
            dma((n_row - 1,)),
            dma((n_row,)),
            dma,
            dma,
            dma,
            dma,
            dma((4,)),
        ],
        compiler_params=pltpu.CompilerParams(
            collective_id=0, has_side_effects=True, vmem_limit_bytes=40 * 1024 * 1024
        ),
        name="mixer",
    )(pin(queries), counts, *map(pin, args[2:4] + weights + args[14:]))
    return pl.pallas_call(
        functools.partial(reader, hsize),
        out_shape=(like((n, width), F32), like((boxes, n), F32)),
        in_specs=[vmem] * 11,
        out_specs=(hbm, hbm),
        scratch_shapes=[
            pltpu.VMEM((n, width), BF),
            pltpu.VMEM((n, width), F32),
            pltpu.VMEM((boxes, n), F32),
            dma((2,)),
        ],
        compiler_params=pltpu.CompilerParams(vmem_limit_bytes=32 * 1024 * 1024),
        name="reader",
    )(*held)


def solution(mesh):
    spread = ("parts", "row", "col")
    return jax.shard_map(
        functools.partial(local, mesh.shape["row"]),
        mesh=mesh,
        in_specs=(P(spread, None), P(spread), P(spread, None), P(spread)) + (P(),) * 12,
        out_specs=(P(spread, None), P(None, spread)),
        check_vma=False,
    )
```

```python
import functools
import math

import jax
import jax.numpy as jnp
from jax import lax
from jax.experimental import pallas as pl
from jax.experimental.pallas import tpu as pltpu
from jax.sharding import PartitionSpec as P

EPS = 1e-06
LANES = 128
TAIL = 16
BF = jnp.bfloat16
F32 = jnp.float32
MESH = pl.DeviceIdType.MESH
DEAD = 64.0


def rms_round(x):
    return (x * lax.rsqrt(jnp.mean(x * x, axis=-1, keepdims=True) + EPS)).astype(BF)


def mm(a, b):
    return jnp.dot(a, b, preferred_element_type=F32)


def mm_t(a, b):
    return lax.dot_general(a, b, (((1,), (1,)), ((), ())), preferred_element_type=F32)


def flip(x):
    return x.astype(F32).T.astype(BF)


def each(n, body):
    if n <= 16:
        for i in range(n):
            body(i)
    else:
        lax.fori_loop(0, n, lambda i, c: (body(i), c)[1], 0)


def twice(w, hsize):
    pair = 2 * hsize
    return jnp.concatenate([w[:, i : i + pair] for i in range(0, w.shape[1], pair) for _ in (0, 1)], axis=1)


def put_queries(w_ref, qt, temp_ref, hsize):
    zero = jnp.zeros((hsize, qt.shape[1]), BF)
    for h in range(w_ref.shape[0]):
        x = qt[h * hsize : (h + 1) * hsize].astype(BF).astype(F32)
        x = x * (temp_ref[h] * (math.log2(math.e) / math.sqrt(hsize)))
        hi = x.astype(BF)
        lo = (x - hi.astype(F32)).astype(BF)
        for j in (0, 1):
            mine = h % 2 == j
            w_ref[h, j * hsize : (j + 1) * hsize, :] = hi if mine else zero
            w_ref[h, (2 + j) * hsize : (3 + j) * hsize, :] = lo if mine else zero


def put_keys(ka_ref, k, live, first):
    for g in range(k.shape[1] // LANES):
        lanes = slice(g * LANES, (g + 1) * LANES)
        ka_ref[g] = jnp.where(live, k[:, lanes], first[:, lanes]).astype(BF)


def put_values(vt_ref, vt, live, hsize):
    flags = jnp.broadcast_to(live.astype(F32), (TAIL, vt.shape[1])).astype(BF)
    for h in range(vt_ref.shape[0]):
        vt_ref[h, :hsize, :] = jnp.where(live, vt[h * hsize : (h + 1) * hsize], 0.0).astype(BF)
        vt_ref[h, hsize:, :] = flags


def attend(w_ref, chunks, tile, tiles, put, refs=(None, None, None)):
    heads = w_ref.shape[0]
    units = [(t, h) for t in range(tiles) for h in range(heads)]
    held = {}

    def keep(kind, u, here, x):
        if refs[kind] is None:
            held[kind, u, here.start] = x
        else:
            refs[kind][u % 2, here] = x

    def back(kind, u, here):
        return held.pop((kind, u, here.start)) if refs[kind] is None else refs[kind][u % 2, here]

    eight = slice(0, 8)
    for u in range(len(units) + 2):
        best = total = None
        if 1 <= u <= len(units):
            top = jnp.max(back(2, u - 1, eight), axis=0, keepdims=True)
        at = 0
        for keys_of, values_of, size in chunks:
            here = slice(at, at + size)
            at += size
            if u < len(units):
                t, h = units[u]
                s = mm(keys_of(h // 2), w_ref[h, :, t * tile : (t + 1) * tile])
                keep(0, u, here, s)
                part = jnp.max(s.reshape(size // 8, 8, tile), axis=0)
                best = part if best is None else jnp.maximum(best, part)
            if 1 <= u <= len(units):
                keep(1, u - 1, here, jnp.exp2(back(0, u - 1, here) - top).astype(BF))
            if u >= 2:
                part = mm(values_of(units[u - 2][1]), back(1, u - 2, here))
                total = part if total is None else total + part
        if u < len(units):
            keep(2, u, eight, best)
        if u >= 2:
            put(*units[u - 2], total)


def mixer(
    n_row, hsize,
    q_hbm, cnt_s, mem_hbm, mask_h, wq_h, wkv_h, wo_h, wqkv_h, swo_h, up_h, down_h, w1_h, w2_h, w3_h, ct_h, st_h,
    x1_v, ws, kas, vts, cnt, swo, up, down, w1, w2, w3,
    q_v, wq, wkv, wo, wqkv,
    mask_s, ct_s, st_s, mem_v, gat, wc, kac, vtc, ctx_v, hn_v, hn_o, s_v, e_v, m_v, ckw, cvw, skw, sqw,
    in_sem, gsend, grecv, csend, crecv, hsend, hrecv, msem,
):
    n, width = q_v.shape
    m_dev = mem_hbm.shape[0]
    row = lax.axis_index("row")
    other = 1 - lax.axis_index("col")

    barrier = pltpu.get_barrier_semaphore()

    def greet(i):
        pl.semaphore_signal(
            barrier, inc=1, device_id={"row": lax.rem(row + 1 + i, n_row)}, device_id_type=MESH
        )

    each(n_row - 1, greet)
    pl.semaphore_signal(barrier, inc=1, device_id={"col": other}, device_id_type=MESH)

    small = [
        pltpu.make_async_copy(a, b, msem.at[i])
        for i, (a, b) in enumerate(
            ((mem_hbm, mem_v), (mask_h, mask_s), (ct_h, ct_s), (st_h, st_s))
        )
    ]
    for load in small:
        load.start()
    pairs = (
        (q_hbm, q_v), (wq_h, wq), (wkv_h, wkv), (wo_h, wo), (wqkv_h, wqkv),
        (swo_h, swo), (up_h, up), (down_h, down), (w1_h, w1), (w2_h, w2), (w3_h, w3),
    )
    loads = [pltpu.make_async_copy(a, b, in_sem.at[i]) for i, (a, b) in enumerate(pairs)]
    for load in loads:
        load.start()

    for load in small:
        load.wait()
    slot = lax.broadcasted_iota(jnp.int32, (m_dev, width), 0)
    flags = jnp.zeros((m_dev, width), jnp.int32)
    for i in range(m_dev):
        flags = jnp.where(slot == i, mask_s[i], flags)
    gat[row] = jnp.where(flags > 0, mem_v[...].astype(F32), DEAD).astype(BF)
    count = cnt_s[0]
    cnt[0] = jnp.full((8, LANES), count, jnp.int32)
    pl.semaphore_wait(barrier, n_row)

    def gather_copy(i):
        return pltpu.make_async_remote_copy(
            src_ref=gat.at[row], dst_ref=gat.at[row],
            send_sem=gsend.at[i], recv_sem=grecv.at[row],
            device_id={"row": lax.rem(row + 1 + i, n_row)}, device_id_type=MESH,
        )

    each(n_row - 1, lambda i: gather_copy(i).start())
    count_copy = pltpu.make_async_remote_copy(
        src_ref=cnt.at[0], dst_ref=cnt.at[1], send_sem=csend, recv_sem=crecv,
        device_id={"col": other}, device_id_type=MESH,
    )
    count_copy.start()

    loads[0].wait()
    loads[1].wait()
    qct = mm_t(flip(wq[...]), rms_round(q_v[...].astype(F32)))
    put_queries(wc, qct, ct_s, hsize)
    loads[2].wait()
    ckw[...] = twice(wkv[:, :width].astype(F32), hsize).astype(BF)
    cvw[...] = flip(wkv[:, width:])
    loads[4].wait()
    skw[...] = twice(wqkv[:, width : 2 * width].astype(F32), hsize).astype(BF)
    sqw[:width] = flip(wqkv[:, :width])
    sqw[width:] = flip(wqkv[:, 2 * width :])
    loads[3].wait()

    def arrived(i):
        j = lax.rem(row + 1 + i, n_row)
        pltpu.make_async_remote_copy(
            src_ref=gat.at[j], dst_ref=gat.at[j],
            send_sem=gsend.at[i], recv_sem=grecv.at[j],
            device_id={"row": j}, device_id_type=MESH,
        ).wait_recv()

    each(n_row - 1, arrived)

    keys = n_row * m_dev
    held = gat[...].reshape(keys, width)
    marks = held[:, :LANES].astype(F32)
    k = mm(held, ckw[...])
    put_keys(kac, k, marks < 0.5 * DEAD, k[0:1])
    put_values(vtc, mm_t(cvw[...], held), marks.T[0:1] < 0.5 * DEAD, hsize)

    size = min(512, keys)
    chunks = [
        (
            lambda g, at=at: kac[g, at : at + size],
            lambda h, at=at: vtc[h, :, at : at + size],
            size,
        )
        for at in range(0, keys, size)
    ]
    lane = lax.broadcasted_iota(jnp.int32, (1, n), 1)

    tile = min(128, n)
    parts = []

    def put_ctx(t, h, total):
        parts.append(total[:hsize] / total[hsize : hsize + 1])
        if len(parts) * hsize == width:
            here = slice(t * tile, (t + 1) * tile)
            whole = jnp.where(lane[:, here] < count, jnp.concatenate(parts, axis=0), 0.0)
            ctx_v[here, :] = whole.T.astype(BF)
            parts.clear()

    attend(wc, chunks, tile, n // tile, put_ctx)

    x1 = q_v[...].astype(F32) + mm(ctx_v[...], wo[...])
    hn_v[...] = rms_round(x1)
    hn_copy = pltpu.make_async_remote_copy(
        src_ref=hn_v, dst_ref=hn_o, send_sem=hsend, recv_sem=hrecv,
        device_id={"col": other}, device_id_type=MESH,
    )
    hn_copy.start()
    x1_v[...] = x1

    k = mm(hn_v[...], skw[...])
    first = k[0:1]
    spot = lax.broadcasted_iota(jnp.int32, (n, LANES), 0)
    put_keys(kas.at[0], k, spot < count, first)
    qvt = mm_t(sqw[...], hn_v[...])
    put_queries(ws, qvt[:width], st_s, hsize)
    put_values(vts.at[0], qvt[width:], lane < count, hsize)
    count_copy.wait()
    hn_copy.wait_recv()
    theirs = cnt[1, 0:1, :]
    put_keys(kas.at[1], mm(hn_o[...], skw[...]), spot < theirs, first)
    put_values(vts.at[1], mm_t(sqw[width:], hn_o[...]), lane < theirs[:, 0:1], hsize)

    for load in loads[5:]:
        load.wait()
    each(n_row - 1, lambda i: gather_copy(i).wait_send())
    hn_copy.wait_send()


def reader(
    hsize,
    cnt_s, x1_v, ws, kas, vts, cnt, swo, up, down, w1, w2, w3,
    feat_ref, box_ref,
    sc_v, out_v, box_v, sems,
):
    n, width = x1_v.shape
    heads = ws.shape[0]
    count = cnt_s[0]
    theirs = jnp.max(cnt[1])
    unit = min(LANES, n)
    half = n // 2
    more = (theirs > count).astype(jnp.int32)
    fewer = jnp.minimum(theirs, count)
    lane = lax.broadcasted_iota(jnp.int32, (1, n), 1)

    def self_rows(rows, size):
        def side(s, upto):
            return (lambda g: kas[s, g, :upto], lambda h: vts[s, h, :, :upto], upto)

        parts = []

        def put(t, h, total):
            parts.append(total[:hsize] / total[hsize : hsize + 1])
            if h == heads - 1:
                here = slice(t * unit, (t + 1) * unit)
                whole = jnp.where(lane[:, here] < count, jnp.concatenate(parts, axis=0), 0.0)
                sc_v[here, :] = whole.T.astype(BF)
                parts.clear()

        attend(ws, [side(more, n), side(1 - more, size)], unit, rows // unit, put)

    @pl.when(count <= half)
    def _():
        sc_v[half:, :] = jnp.zeros((n - half, width), BF)

    for i in range(n // unit):
        size = (i + 1) * unit
        chosen = (fewer - 1) // unit == i

        @pl.when(jnp.logical_and(chosen, count > half))
        def _():
            self_rows(n, size)

        if size % (2 * unit) == 0:

            @pl.when(jnp.logical_and((fewer - 1) // (2 * unit) == i // 2, count <= half))
            def _():
                self_rows(half, size)

    x2 = x1_v[...] + mm(sc_v[...], swo[...])
    hn2 = rms_round(x2)
    ff = up.shape[1]
    step = min(256, ff)
    x3 = x2
    for f in range(0, ff, step):
        upper = jnp.maximum(mm(hn2, up[:, f : f + step]), 0.0).astype(BF)
        x3 = x3 + mm(upper, down[f : f + step, :])
    alive = lax.broadcasted_iota(jnp.int32, (n, width), 0) < count
    out_v[...] = jnp.where(alive, x3, 0.0)
    put = pltpu.make_async_copy(out_v, feat_ref, sems.at[0])
    put.start()
    hn3 = rms_round(x3)
    b1 = jnp.maximum(mm(hn3, w1[...]), 0.0).astype(BF)
    b2 = jnp.maximum(mm(b1, w2[...]), 0.0).astype(BF)
    z = lax.dot_general(w3[...], b2, (((1,), (1,)), ((), ())), preferred_element_type=F32)
    box = 1.0 / (1.0 + jnp.exp(-z))
    box_v[...] = jnp.where(lax.broadcasted_iota(jnp.int32, box.shape, 1) < count, box, 0.0)
    put_box = pltpu.make_async_copy(box_v, box_ref, sems.at[1])
    put_box.start()
    put.wait()
    put_box.wait()


def pin(x):
    return pltpu.with_memory_space_constraint(x, pltpu.HBM)


def local(n_row, *args):
    queries, counts, memory, mem_mask = args[:4]
    weights = args[4:13] + (args[13].T,)
    n, width = queries.shape
    m_dev = memory.shape[0]
    heads = args[14].shape[0]
    hsize = width // heads
    keys = n_row * m_dev
    groups = 2 * width // LANES
    hbm = pl.BlockSpec(memory_space=pltpu.HBM)
    smem = pl.BlockSpec(memory_space=pltpu.SMEM)
    vmem = pl.BlockSpec(memory_space=pltpu.VMEM)
    dma = pltpu.SemaphoreType.DMA
    boxes = weights[-1].shape[0]
    like = jax.ShapeDtypeStruct
    held = pl.pallas_call(
        functools.partial(mixer, n_row, hsize),
        out_shape=(
            like((n, width), F32),
            like((heads, LANES, n), BF),
            like((2, groups, n, LANES), BF),
            like((2, heads, hsize + TAIL, n), BF),
            like((2, 8, LANES), jnp.int32),
        )
        + tuple(like(w.shape, BF) for w in weights[4:]),
        in_specs=[hbm, smem] + [hbm] * 14,
        out_specs=(vmem,) * (5 + len(weights[4:])),
        scratch_shapes=[pltpu.VMEM(queries.shape, BF)]
        + [pltpu.VMEM(w.shape, BF) for w in weights[:4]]
        + [
            pltpu.SMEM(mem_mask.shape, jnp.int32),
            pltpu.SMEM((heads,), F32),
            pltpu.SMEM((heads,), F32),
            pltpu.VMEM(memory.shape, BF),
            pltpu.VMEM((n_row, m_dev, width), BF),
            pltpu.VMEM((heads, LANES, n), BF),
            pltpu.VMEM((groups, keys, LANES), BF),
            pltpu.VMEM((heads, hsize + TAIL, keys), BF),
            pltpu.VMEM((n, width), BF),
            pltpu.VMEM((n, width), BF),
            pltpu.VMEM((n, width), BF),
            pltpu.VMEM((2, keys, n), F32),
            pltpu.VMEM((2, keys, n), BF),
            pltpu.VMEM((2, 8, n), F32),
            pltpu.VMEM((width, 2 * width), BF),
            pltpu.VMEM((width, width), BF),
            pltpu.VMEM((width, 2 * width), BF),
            pltpu.VMEM((2 * width, width), BF),
            dma((11,)),
            dma((n_row - 1,)),
            dma((n_row,)),
            dma,
            dma,
            dma,
            dma,
            dma((4,)),
        ],
        compiler_params=pltpu.CompilerParams(
            collective_id=0, has_side_effects=True, vmem_limit_bytes=40 * 1024 * 1024
        ),
        name="mixer",
    )(pin(queries), counts, *map(pin, args[2:4] + weights + args[14:]))
    return pl.pallas_call(
        functools.partial(reader, hsize),
        out_shape=(like((n, width), F32), like((boxes, n), F32)),
        in_specs=[smem] + [vmem] * 11,
        out_specs=(hbm, hbm),
        scratch_shapes=[
            pltpu.VMEM((n, width), BF),
            pltpu.VMEM((n, width), F32),
            pltpu.VMEM((boxes, n), F32),
            dma((2,)),
        ],
        compiler_params=pltpu.CompilerParams(vmem_limit_bytes=32 * 1024 * 1024),
        name="reader",
    )(counts, *held)


def solution(mesh):
    spread = ("parts", "row", "col")
    return jax.shard_map(
        functools.partial(local, mesh.shape["row"]),
        mesh=mesh,
        in_specs=(P(spread, None), P(spread), P(spread, None), P(spread)) + (P(),) * 12,
        out_specs=(P(spread, None), P(None, spread)),
        check_vma=False,
    )
```

```python
import functools
import math

import jax
import jax.numpy as jnp
from jax import lax
from jax.experimental import pallas as pl
from jax.experimental.pallas import tpu as pltpu
from jax.sharding import PartitionSpec as P

EPS = 1e-06
LANES = 128
TAIL = 16
BF = jnp.bfloat16
F32 = jnp.float32
MESH = pl.DeviceIdType.MESH
DEAD = 64.0


def rms_round(x):
    return (x * lax.rsqrt(jnp.mean(x * x, axis=-1, keepdims=True) + EPS)).astype(BF)


def mm(a, b):
    return jnp.dot(a, b, preferred_element_type=F32)


def mm_t(a, b):
    return lax.dot_general(a, b, (((1,), (1,)), ((), ())), preferred_element_type=F32)


def flip(x):
    return x.astype(F32).T.astype(BF)


def each(n, body):
    if n <= 16:
        for i in range(n):
            body(i)
    else:
        lax.fori_loop(0, n, lambda i, c: (body(i), c)[1], 0)


def twice(w, hsize):
    pair = 2 * hsize
    return jnp.concatenate([w[:, i : i + pair] for i in range(0, w.shape[1], pair) for _ in (0, 1)], axis=1)


def put_queries(w_ref, qt, temp_ref, hsize):
    zero = jnp.zeros((hsize, qt.shape[1]), BF)
    for h in range(w_ref.shape[0]):
        x = qt[h * hsize : (h + 1) * hsize].astype(BF).astype(F32)
        x = x * (temp_ref[h] * (math.log2(math.e) / math.sqrt(hsize)))
        hi = x.astype(BF)
        lo = (x - hi.astype(F32)).astype(BF)
        for j in (0, 1):
            mine = h % 2 == j
            w_ref[h, j * hsize : (j + 1) * hsize, :] = hi if mine else zero
            w_ref[h, (2 + j) * hsize : (3 + j) * hsize, :] = lo if mine else zero


def put_keys(ka_ref, k, live, first):
    for g in range(k.shape[1] // LANES):
        lanes = slice(g * LANES, (g + 1) * LANES)
        ka_ref[g] = jnp.where(live, k[:, lanes], first[:, lanes]).astype(BF)


def put_values(vt_ref, vt, live, hsize):
    flags = jnp.broadcast_to(live.astype(F32), (TAIL, vt.shape[1])).astype(BF)
    for h in range(vt_ref.shape[0]):
        vt_ref[h, :hsize, :] = jnp.where(live, vt[h * hsize : (h + 1) * hsize], 0.0).astype(BF)
        vt_ref[h, hsize:, :] = flags


def attend(w_ref, chunks, tile, tiles, put, refs=(None, None, None)):
    heads = w_ref.shape[0]
    units = [(t, h) for t in range(tiles) for h in range(heads)]
    held = {}

    def keep(kind, u, here, x):
        if refs[kind] is None:
            held[kind, u, here.start] = x
        else:
            refs[kind][u % 2, here] = x

    def back(kind, u, here):
        return held.pop((kind, u, here.start)) if refs[kind] is None else refs[kind][u % 2, here]

    eight = slice(0, 8)
    for u in range(len(units) + 2):
        best = total = None
        if 1 <= u <= len(units):
            top = jnp.max(back(2, u - 1, eight), axis=0, keepdims=True)
        at = 0
        for keys_of, values_of, size in chunks:
            here = slice(at, at + size)
            at += size
            if u < len(units):
                t, h = units[u]
                s = mm(keys_of(h // 2), w_ref[h, :, t * tile : (t + 1) * tile])
                keep(0, u, here, s)
                part = jnp.max(s.reshape(size // 8, 8, tile), axis=0)
                best = part if best is None else jnp.maximum(best, part)
            if 1 <= u <= len(units):
                keep(1, u - 1, here, jnp.exp2(back(0, u - 1, here) - top).astype(BF))
            if u >= 2:
                part = mm(values_of(units[u - 2][1]), back(1, u - 2, here))
                total = part if total is None else total + part
        if u < len(units):
            keep(2, u, eight, best)
        if u >= 2:
            put(*units[u - 2], total)


def mixer(
    n_row, hsize,
    q_hbm, cnt_s, mem_hbm, mask_h, wq_h, wkv_h, wo_h, wqkv_h, swo_h, up_h, down_h, w1_h, w2_h, w3_h, ct_h, st_h,
    x1_v, ws, kas, vts, cnt, swo, up, down, w1, w2, w3,
    q_v, wq, wkv, wo, wqkv,
    mask_s, ct_s, st_s, mem_v, gat, wc, kac, vtc, ctx_v, hn_v, hn_o, s_v, e_v, m_v, ckw, cvw, skw, sqw,
    in_sem, gsend, grecv, csend, crecv, hsend, hrecv, msem,
):
    n, width = q_v.shape
    m_dev = mem_hbm.shape[0]
    row = lax.axis_index("row")
    other = 1 - lax.axis_index("col")

    barrier = pltpu.get_barrier_semaphore()

    def greet(i):
        pl.semaphore_signal(
            barrier, inc=1, device_id={"row": lax.rem(row + 1 + i, n_row)}, device_id_type=MESH
        )

    each(n_row - 1, greet)
    pl.semaphore_signal(barrier, inc=1, device_id={"col": other}, device_id_type=MESH)

    small = [
        pltpu.make_async_copy(a, b, msem.at[i])
        for i, (a, b) in enumerate(
            ((mem_hbm, mem_v), (mask_h, mask_s), (ct_h, ct_s), (st_h, st_s))
        )
    ]
    for load in small:
        load.start()
    pairs = (
        (q_hbm, q_v), (wq_h, wq), (wkv_h, wkv), (wo_h, wo), (wqkv_h, wqkv),
        (swo_h, swo), (up_h, up), (down_h, down), (w1_h, w1), (w2_h, w2), (w3_h, w3),
    )
    loads = [pltpu.make_async_copy(a, b, in_sem.at[i]) for i, (a, b) in enumerate(pairs)]
    for load in loads:
        load.start()

    for load in small:
        load.wait()
    slot = lax.broadcasted_iota(jnp.int32, (m_dev, width), 0)
    flags = jnp.zeros((m_dev, width), jnp.int32)
    for i in range(m_dev):
        flags = jnp.where(slot == i, mask_s[i], flags)
    gat[row] = jnp.where(flags > 0, mem_v[...].astype(F32), DEAD).astype(BF)
    count = cnt_s[0]
    cnt[0] = jnp.full((8, LANES), count, jnp.int32)
    pl.semaphore_wait(barrier, n_row)

    def gather_copy(i):
        step = 1 + lax.rem(i + n_row // 2 - 1, n_row - 1)
        return pltpu.make_async_remote_copy(
            src_ref=gat.at[row], dst_ref=gat.at[row],
            send_sem=gsend.at[i], recv_sem=grecv.at[row],
            device_id={"row": lax.rem(row + step, n_row)}, device_id_type=MESH,
        )

    each(n_row - 1, lambda i: gather_copy(i).start())
    count_copy = pltpu.make_async_remote_copy(
        src_ref=cnt.at[0], dst_ref=cnt.at[1], send_sem=csend, recv_sem=crecv,
        device_id={"col": other}, device_id_type=MESH,
    )
    count_copy.start()

    loads[0].wait()
    loads[1].wait()
    qct = mm_t(flip(wq[...]), rms_round(q_v[...].astype(F32)))
    put_queries(wc, qct, ct_s, hsize)
    loads[2].wait()
    ckw[...] = twice(wkv[:, :width].astype(F32), hsize).astype(BF)
    cvw[...] = flip(wkv[:, width:])
    loads[4].wait()
    skw[...] = twice(wqkv[:, width : 2 * width].astype(F32), hsize).astype(BF)
    sqw[:width] = flip(wqkv[:, :width])
    sqw[width:] = flip(wqkv[:, 2 * width :])
    loads[3].wait()

    def arrived(i):
        j = lax.rem(row + 1 + i, n_row)
        pltpu.make_async_remote_copy(
            src_ref=gat.at[j], dst_ref=gat.at[j],
            send_sem=gsend.at[i], recv_sem=grecv.at[j],
            device_id={"row": j}, device_id_type=MESH,
        ).wait_recv()

    each(n_row - 1, arrived)

    keys = n_row * m_dev
    held = gat[...].reshape(keys, width)
    marks = held[:, :LANES].astype(F32)
    k = mm(held, ckw[...])
    put_keys(kac, k, marks < 0.5 * DEAD, k[0:1])
    put_values(vtc, mm_t(cvw[...], held), marks.T[0:1] < 0.5 * DEAD, hsize)

    size = min(512, keys)
    chunks = [
        (
            lambda g, at=at: kac[g, at : at + size],
            lambda h, at=at: vtc[h, :, at : at + size],
            size,
        )
        for at in range(0, keys, size)
    ]
    lane = lax.broadcasted_iota(jnp.int32, (1, n), 1)

    tile = min(128, n)
    parts = []

    def put_ctx(t, h, total):
        parts.append(total[:hsize] / total[hsize : hsize + 1])
        if len(parts) * hsize == width:
            here = slice(t * tile, (t + 1) * tile)
            whole = jnp.where(lane[:, here] < count, jnp.concatenate(parts, axis=0), 0.0)
            ctx_v[here, :] = whole.T.astype(BF)
            parts.clear()

    attend(wc, chunks, tile, n // tile, put_ctx)

    x1 = q_v[...].astype(F32) + mm(ctx_v[...], wo[...])
    hn_v[...] = rms_round(x1)
    hn_copy = pltpu.make_async_remote_copy(
        src_ref=hn_v, dst_ref=hn_o, send_sem=hsend, recv_sem=hrecv,
        device_id={"col": other}, device_id_type=MESH,
    )
    hn_copy.start()
    x1_v[...] = x1

    k = mm(hn_v[...], skw[...])
    first = k[0:1]
    spot = lax.broadcasted_iota(jnp.int32, (n, LANES), 0)
    put_keys(kas.at[0], k, spot < count, first)
    qvt = mm_t(sqw[...], hn_v[...])
    put_queries(ws, qvt[:width], st_s, hsize)
    put_values(vts.at[0], qvt[width:], lane < count, hsize)
    count_copy.wait()
    hn_copy.wait_recv()
    theirs = cnt[1, 0:1, :]
    put_keys(kas.at[1], mm(hn_o[...], skw[...]), spot < theirs, first)
    put_values(vts.at[1], mm_t(sqw[width:], hn_o[...]), lane < theirs[:, 0:1], hsize)

    for load in loads[5:]:
        load.wait()
    each(n_row - 1, lambda i: gather_copy(i).wait_send())
    hn_copy.wait_send()


def reader(
    hsize,
    cnt_s, x1_v, ws, kas, vts, cnt, swo, up, down, w1, w2, w3,
    feat_ref, box_ref,
    sc_v, out_v, box_v, sems,
):
    n, width = x1_v.shape
    heads = ws.shape[0]
    count = cnt_s[0]
    theirs = jnp.max(cnt[1])
    unit = min(LANES, n)
    half = n // 2
    more = (theirs > count).astype(jnp.int32)
    fewer = jnp.minimum(theirs, count)
    lane = lax.broadcasted_iota(jnp.int32, (1, n), 1)

    def self_rows(rows, size):
        def side(s, upto):
            return (lambda g: kas[s, g, :upto], lambda h: vts[s, h, :, :upto], upto)

        parts = []

        def put(t, h, total):
            parts.append(total[:hsize] / total[hsize : hsize + 1])
            if h == heads - 1:
                here = slice(t * unit, (t + 1) * unit)
                whole = jnp.where(lane[:, here] < count, jnp.concatenate(parts, axis=0), 0.0)
                sc_v[here, :] = whole.T.astype(BF)
                parts.clear()

        attend(ws, [side(more, n), side(1 - more, size)], unit, rows // unit, put)

    @pl.when(count <= half)
    def _():
        sc_v[half:, :] = jnp.zeros((n - half, width), BF)

    for i in range(n // unit):
        size = (i + 1) * unit
        chosen = (fewer - 1) // unit == i

        @pl.when(jnp.logical_and(chosen, count > half))
        def _():
            self_rows(n, size)

        if size % (2 * unit) == 0:

            @pl.when(jnp.logical_and((fewer - 1) // (2 * unit) == i // 2, count <= half))
            def _():
                self_rows(half, size)

    x2 = x1_v[...] + mm(sc_v[...], swo[...])
    hn2 = rms_round(x2)
    ff = up.shape[1]
    step = min(256, ff)
    x3 = x2
    for f in range(0, ff, step):
        upper = jnp.maximum(mm(hn2, up[:, f : f + step]), 0.0).astype(BF)
        x3 = x3 + mm(upper, down[f : f + step, :])
    alive = lax.broadcasted_iota(jnp.int32, (n, width), 0) < count
    out_v[...] = jnp.where(alive, x3, 0.0)
    put = pltpu.make_async_copy(out_v, feat_ref, sems.at[0])
    put.start()
    hn3 = rms_round(x3)
    b1 = jnp.maximum(mm(hn3, w1[...]), 0.0).astype(BF)
    b2 = jnp.maximum(mm(b1, w2[...]), 0.0).astype(BF)
    z = lax.dot_general(w3[...], b2, (((1,), (1,)), ((), ())), preferred_element_type=F32)
    box = 1.0 / (1.0 + jnp.exp(-z))
    box_v[...] = jnp.where(lax.broadcasted_iota(jnp.int32, box.shape, 1) < count, box, 0.0)
    put_box = pltpu.make_async_copy(box_v, box_ref, sems.at[1])
    put_box.start()
    put.wait()
    put_box.wait()


def pin(x):
    return pltpu.with_memory_space_constraint(x, pltpu.HBM)


def local(n_row, *args):
    queries, counts, memory, mem_mask = args[:4]
    weights = args[4:13] + (args[13].T,)
    n, width = queries.shape
    m_dev = memory.shape[0]
    heads = args[14].shape[0]
    hsize = width // heads
    keys = n_row * m_dev
    groups = 2 * width // LANES
    hbm = pl.BlockSpec(memory_space=pltpu.HBM)
    smem = pl.BlockSpec(memory_space=pltpu.SMEM)
    vmem = pl.BlockSpec(memory_space=pltpu.VMEM)
    dma = pltpu.SemaphoreType.DMA
    boxes = weights[-1].shape[0]
    like = jax.ShapeDtypeStruct
    held = pl.pallas_call(
        functools.partial(mixer, n_row, hsize),
        out_shape=(
            like((n, width), F32),
            like((heads, LANES, n), BF),
            like((2, groups, n, LANES), BF),
            like((2, heads, hsize + TAIL, n), BF),
            like((2, 8, LANES), jnp.int32),
        )
        + tuple(like(w.shape, BF) for w in weights[4:]),
        in_specs=[hbm, smem] + [hbm] * 14,
        out_specs=(vmem,) * (5 + len(weights[4:])),
        scratch_shapes=[pltpu.VMEM(queries.shape, BF)]
        + [pltpu.VMEM(w.shape, BF) for w in weights[:4]]
        + [
            pltpu.SMEM(mem_mask.shape, jnp.int32),
            pltpu.SMEM((heads,), F32),
            pltpu.SMEM((heads,), F32),
            pltpu.VMEM(memory.shape, BF),
            pltpu.VMEM((n_row, m_dev, width), BF),
            pltpu.VMEM((heads, LANES, n), BF),
            pltpu.VMEM((groups, keys, LANES), BF),
            pltpu.VMEM((heads, hsize + TAIL, keys), BF),
            pltpu.VMEM((n, width), BF),
            pltpu.VMEM((n, width), BF),
            pltpu.VMEM((n, width), BF),
            pltpu.VMEM((2, keys, n), F32),
            pltpu.VMEM((2, keys, n), BF),
            pltpu.VMEM((2, 8, n), F32),
            pltpu.VMEM((width, 2 * width), BF),
            pltpu.VMEM((width, width), BF),
            pltpu.VMEM((width, 2 * width), BF),
            pltpu.VMEM((2 * width, width), BF),
            dma((11,)),
            dma((n_row - 1,)),
            dma((n_row,)),
            dma,
            dma,
            dma,
            dma,
            dma((4,)),
        ],
        compiler_params=pltpu.CompilerParams(
            collective_id=0, has_side_effects=True, vmem_limit_bytes=40 * 1024 * 1024
        ),
        name="mixer",
    )(pin(queries), counts, *map(pin, args[2:4] + weights + args[14:]))
    return pl.pallas_call(
        functools.partial(reader, hsize),
        out_shape=(like((n, width), F32), like((boxes, n), F32)),
        in_specs=[smem] + [vmem] * 11,
        out_specs=(hbm, hbm),
        scratch_shapes=[
            pltpu.VMEM((n, width), BF),
            pltpu.VMEM((n, width), F32),
            pltpu.VMEM((boxes, n), F32),
            dma((2,)),
        ],
        compiler_params=pltpu.CompilerParams(vmem_limit_bytes=32 * 1024 * 1024),
        name="reader",
    )(counts, *held)


def solution(mesh):
    spread = ("parts", "row", "col")
    return jax.shard_map(
        functools.partial(local, mesh.shape["row"]),
        mesh=mesh,
        in_specs=(P(spread, None), P(spread), P(spread, None), P(spread)) + (P(),) * 12,
        out_specs=(P(spread, None), P(None, spread)),
        check_vma=False,
    )
```
